32 devices in a mesh: blk: 8 (over y, x, core), expert: 4 (over z).
Axes of the slice: x: 2, y: 2, z: 4, core: 2. Of those that a mesh axis runs over, the one named last changes fastest.
Arguments:
- residual: bfloat16 [2048, 4096], P('blk', 'expert'), may hold values from -3 to 3
- queries: bfloat16 [2048, 2048], P('blk', 'expert'), may hold values from -8 to 8
- key_cache: bfloat16 [2048, 1024], P('blk', 'expert'), may hold values from -8 to 8
- value_cache: bfloat16 [2048, 1024], P('blk', 'expert'), may hold values from -6 to 6
- segments: int32 [2048], replicated, may hold values from 0 to 3, never falling along the last dimension, each value on 1 to 1536 neighbouring positions
- routes: int32 [2048, 2], P('blk'), may hold values from 0 to 3, all different within a row; in each aligned block of 256 rows (0 to 255, 256 to 511, ...) at most 144 rows name the same one
- w_out: bfloat16 [2048, 4096], P('expert'), may hold values from -0.125 to 0.125
- norm_gain: float32 [4096], replicated, may hold values from 0.5 to 1.5
- w_router: bfloat16 [4096, 4], replicated, may hold values from -0.09375 to 0.09375
- w_gate: bfloat16 [4, 4096, 14336], P('expert', None, 'blk'), may hold values from -0.09375 to 0.09375
- w_up: bfloat16 [4, 4096, 14336], P('expert', None, 'blk'), may hold values from -0.09375 to 0.09375
- w_down: bfloat16 [4, 14336, 4096], P('expert', 'blk'), may hold values from -0.046875 to 0.046875
Outputs:
- layer_out: bfloat16 [2048, 4096], P(('blk', 'expert'))
The draws below stay inside these ranges and needn't reach their ends.
Inputs may be any that keep to these rules, and one draw needn't show every extreme that they name: `segments`: segment ids never fall; one document holds exactly 1536 tokens and none holds more. `routes`: A token's 2 experts differ. In each aligned block of 256 rows (the tokens of one index of blk) no expert is named by more than 144 rows, a bound that some block reaches.
All inputs are finite; a program needn't handle non-finite values.
Results may differ from the reference program's by a relative error of at most 0.019.
Values may be sent and summed in bfloat16 or wider, within the bound.
A program may use at most 192 MiB of HBM per device.

```python
import math
import jax
import jax.numpy as jnp
import numpy as np
from jax import lax

D = 4096
H = 16
KVH = 8
HD = 128
FF = 14336
TOP = 2
S_BLK = 256
SEGS = 4
EXPERTS = 4
TOKENS = 2048
LONGEST = 1536
CAP = 144
N_BLK = 8


def draw_queries(key, part):
    values_out = 1.5 * jax.random.normal(jax.random.fold_in(key, 22), (TOKENS, H * HD), jnp.float32)
    return jnp.clip(values_out, -8.0, 8.0).astype(jnp.bfloat16)


def draw_key_cache(key, part):
    values_out = 1.2 * jax.random.normal(jax.random.fold_in(key, 33), (TOKENS, KVH * HD), jnp.float32)
    return jnp.clip(values_out, -8.0, 8.0).astype(jnp.bfloat16)


def block_levels(stream_key, dims, shards, least, largest):
    def one(dim, blocks):
        steps = jax.random.uniform(jax.random.fold_in(jax.random.fold_in(stream_key, 6), dim), (blocks,), jnp.float32, least / len(shards), largest / len(shards))
        return jnp.repeat(jnp.exp(steps), dims[dim] // blocks).reshape((-1,) + (1,) * (len(dims) - dim - 1))

    loudness = one(*shards[0])
    for cut in shards[1:]:
        loudness = loudness * one(*cut)
    return loudness


def profile(number_of, total, bound, lean):
    loads = [(1 << 20) // math.isqrt(standing ** lean) + 1 for standing in range(2, number_of + 1)]
    rest, given = total - bound - (number_of - 1), [1] * (number_of - 1)
    while rest > 0:
        movable = [i for i in range(number_of - 1) if given[i] < bound]
        pool, left = sum([loads[i] for i in movable]), rest
        for i in movable:
            addition = min(bound - given[i], max(1, left * loads[i] // pool), rest)
            given[i] = given[i] + addition
            rest = rest - addition
    return np.array([bound] + given)


def uneven(rng, count, total, most, slope):
    if count == 2:
        one = jax.random.randint(rng, (), max(1, total - most), min(most, total - 1) + 1)
        return jnp.stack([one, total - one])
    sizes = jnp.asarray(profile(count, total, most, slope), jnp.int32)
    couples = (count - 1) // 2
    donor, sink = sizes[1:1 + 2 * couples:2], sizes[2:2 + 2 * couples:2]
    room = jnp.minimum(donor - 1, most - sink)
    passed = jax.random.randint(jax.random.fold_in(rng, 1), (couples,), 0, 1 << 20) % (room + 1)
    sizes = sizes.at[1:1 + 2 * couples:2].set(donor - passed).at[2:2 + 2 * couples:2].set(sink + passed)
    return sizes[jax.random.permutation(jax.random.fold_in(rng, 2), count)]


def deal_out(own_key, own, number, rows, count, top, most, lean):
    sequence = jax.random.permutation(own_key, count)
    packed, ordinary = load_shares(count, rows * top, most, lean, True), load_shares(count, rows * top, most, lean, False)
    places = jnp.arange(count)

    def named(tallies, turn):
        used = int((tallies > 0).sum())
        fixed = max(1, used // 4)
        moved = fixed + (places - fixed + turn * (used - fixed)) % max(1, count - fixed)
        return jnp.zeros((count,), jnp.int32).at[sequence[jnp.where(places < fixed, places, moved)]].set(jnp.asarray(tallies, jnp.int32))

    tallies = jnp.where(number % 4 == 0, named(packed, number // 4), named(ordinary, number - number // 4 - 1))
    mixed = jax.random.permutation(jax.random.fold_in(own, 3), count)
    source_of, sink = mixed[0:count // 2 * 2:2], mixed[1:count // 2 * 2:2]
    margin = jnp.minimum(tallies[source_of] - 1, most - tallies[sink]) // 2
    margin = jnp.where((source_of == sequence[0]) | (sink == sequence[0]) | (tallies[sink] == 0), 0, jnp.maximum(margin, 0))
    moved = jax.random.randint(jax.random.fold_in(own, 4), (count // 2,), 0, 1 << 20) % (margin + 1)
    tallies = tallies.at[source_of].add(-moved).at[sink].add(moved)
    members = jnp.searchsorted(jnp.cumsum(tallies), jnp.arange(rows * top), side="right").astype(jnp.int32)
    grid = members.reshape(top, rows).T
    grid = grid[jax.random.permutation(jax.random.fold_in(own, 1), rows)]
    turn = jax.random.randint(jax.random.fold_in(own, 2), (rows, 1), 0, top)
    return jnp.take_along_axis(grid, (jnp.arange(top)[None, :] + turn) % top, axis=1)


def load_shares(number_of, total, most, lean, full):
    loads = [(1 << 20) // math.isqrt(grade ** lean) + 1 for grade in range(1, number_of + 1)]
    largest = most if full else min(most, max(-(-total // number_of), total * loads[0] // sum(loads)))
    least = 1 if total - largest >= number_of - 1 else 0
    counts, surplus = [largest] + [least] * (number_of - 1), total - largest - least * (number_of - 1)
    while surplus > 0:
        candidates = [i for i in range(1, number_of) if counts[i] < largest] or [i for i in range(1, number_of) if counts[i] < most]
        pool, budget = sum([loads[i] for i in candidates]), surplus
        for i in candidates:
            addition = min(most - counts[i], max(1, budget * loads[i] // pool), surplus)
            counts[i] = counts[i] + addition
            surplus = surplus - addition
    return np.array(counts)


def bell_draw(rng, extent, spread, reach, pieces=(), held_as=jnp.bfloat16):
    result = jax.random.normal(rng, extent, jnp.float32) * spread
    if len(pieces) > 0:
        result = block_levels(rng, extent, pieces, -0.22, 0.18) * result
    return jnp.clip(result, min=-reach, max=reach).astype(held_as)


def setup_inputs(seed: int = 0) -> dict:
    keys = jax.random.split(jax.random.key(seed), 13)
    residual = bell_draw(keys[0], (TOKENS, D), 0.5, 3.0, ((0, 8), (1, 4)))
    queries = draw_queries(jax.random.fold_in(keys[12], 71), 0)
    key_cache = draw_key_cache(jax.random.fold_in(keys[12], 71), 0)
    value_cache = bell_draw(keys[3], (TOKENS, KVH * HD), 1.0, 6.0, ((0, 8), (1, 4)))
    segments = jnp.searchsorted(jnp.cumsum(uneven(keys[4], SEGS, TOKENS, LONGEST, 2)), jnp.arange(TOKENS), side="right").astype(jnp.int32)
    routes_keys = jax.random.split(jax.random.fold_in(keys[5], 1), TOKENS // S_BLK)
    routes_turns = jax.random.permutation(jax.random.fold_in(keys[5], 3), TOKENS // S_BLK)
    routes = jax.vmap(lambda own, number: deal_out(jax.random.fold_in(keys[5], 2), own, number, S_BLK, EXPERTS, TOP, CAP, 1))(routes_keys, routes_turns).reshape((TOKENS, TOP))
    w_out = bell_draw(keys[6], (H * HD, D), (H * HD) ** -0.5, 0.125, ((0, 4),))
    norm_gain = jnp.clip(1.0 + 0.1 * jax.random.normal(keys[7], (D,), jnp.float32), 0.5, 1.5)
    w_router = bell_draw(keys[8], (D, EXPERTS), D ** -0.5, 0.09375)
    w_gate = bell_draw(keys[9], (EXPERTS, D, FF), D ** -0.5, 0.09375, ((0, 4), (2, 8)))
    w_up = bell_draw(keys[10], (EXPERTS, D, FF), D ** -0.5, 0.09375, ((0, 4), (2, 8)))
    w_down = bell_draw(keys[11], (EXPERTS, FF, D), FF ** -0.5, 0.046875, ((0, 4), (1, 8)))
    return dict(residual=residual, queries=queries, key_cache=key_cache, value_cache=value_cache, segments=segments, routes=routes, w_out=w_out, norm_gain=norm_gain, w_router=w_router, w_gate=w_gate, w_up=w_up, w_down=w_down)


def attend_head(operands, allowed):
    q_group, k_group, v_group = operands
    score_scale = 1.0 / math.sqrt(HD)
    scores = jnp.einsum('tgd,sd->gts', q_group.astype(jnp.float32), k_group.astype(jnp.float32)) * score_scale
    masked = jnp.where(allowed[None, :, :], scores, -1e+30)
    row_max = lax.optimization_barrier(jnp.max(masked, axis=-1, keepdims=True))
    weights = jnp.where(allowed[None, :, :], jnp.exp(masked - row_max), 0.0)
    denominator = lax.optimization_barrier(jnp.sum(weights, axis=-1))
    weight_low = weights.astype(jnp.bfloat16)
    summed = jnp.einsum('gts,sd->tgd', weight_low.astype(jnp.float32), v_group.astype(jnp.float32))
    return (summed / jnp.transpose(denominator)[:, :, None]).astype(jnp.bfloat16)

def reference(residual, queries, key_cache, value_cache, segments, routes, w_out, norm_gain, w_router, w_gate, w_up, w_down):
    q_per_kv = H // KVH
    position = jnp.arange(TOKENS, dtype=jnp.int32)
    allowed = (segments[:, None] == segments[None, :]) & (position[None, :] <= position[:, None])
    q_four = jnp.transpose(queries.reshape(TOKENS, KVH, q_per_kv, HD), (1, 0, 2, 3))
    k_three = jnp.transpose(key_cache.reshape(TOKENS, KVH, HD), (1, 0, 2))
    v_three = jnp.transpose(value_cache.reshape(TOKENS, KVH, HD), (1, 0, 2))
    attended = lax.map(partial_attend(allowed), (q_four, k_three, v_three))
    attended = jnp.transpose(attended, (1, 0, 2, 3)).reshape(TOKENS, H * HD)
    stream = residual.astype(jnp.float32) + jnp.dot(attended, w_out, preferred_element_type=jnp.float32)
    normed = (stream * lax.rsqrt(lax.optimization_barrier(jnp.mean(stream * stream, axis=-1, keepdims=True)) + 1e-05) * norm_gain).astype(jnp.bfloat16)
    gate_score = jax.nn.sigmoid(jnp.dot(normed, w_router, preferred_element_type=jnp.float32))
    chosen = jnp.take_along_axis(gate_score, routes, axis=1)
    mixing = chosen / lax.optimization_barrier(jnp.sum(chosen, axis=-1, keepdims=True))
    ff_part = FF // N_BLK
    slot_count = N_BLK * CAP
    slot_base = (jnp.arange(N_BLK, dtype=jnp.int32) * CAP)[:, None]
    mixture = jnp.zeros((TOKENS, D), jnp.float32)
    for expert_id in range(EXPERTS):
        chosen_here = routes == expert_id
        routed = jnp.any(chosen_here, axis=-1)
        share_w = lax.optimization_barrier(jnp.sum(jnp.where(chosen_here, mixing, 0.0), axis=-1))
        slot_index = (jnp.cumsum(routed.reshape(N_BLK, S_BLK).astype(jnp.int32), axis=1) - 1 + slot_base).reshape(TOKENS)
        target = jnp.where(routed, slot_index, slot_count).astype(jnp.int32)
        token_slot = jnp.zeros((slot_count,), jnp.int32).at[target].set(position, mode='drop')
        gathered = normed[token_slot]
        gate = jnp.dot(gathered, w_gate[expert_id], preferred_element_type=jnp.float32)
        up_proj = jnp.dot(gathered, w_up[expert_id], preferred_element_type=jnp.float32)
        hidden = (jax.nn.silu(gate) * up_proj).astype(jnp.bfloat16)
        partials = jnp.einsum('rnf,nfd->nrd', hidden.reshape(slot_count, N_BLK, ff_part).astype(jnp.float32), w_down[expert_id].reshape(N_BLK, ff_part, D).astype(jnp.float32))
        rounded = lax.optimization_barrier(partials.astype(jnp.bfloat16)).astype(jnp.float32)
        expert_out = lax.optimization_barrier(jnp.sum(rounded, axis=0))
        picked = jnp.clip(slot_index, 0, slot_count - 1).astype(jnp.int32)
        mixture = mixture + share_w[:, None] * expert_out[picked]
    return (stream + mixture).astype(jnp.bfloat16)

def partial_attend(allowed):

    def attend_one(operands):
        return attend_head(operands, allowed)
    return attend_one
```

```python
import functools
import math

import jax
import jax.numpy as jnp
from jax import lax
from jax.experimental import pallas as pl
from jax.experimental.pallas import tpu as pltpu
from jax.sharding import PartitionSpec as P

H = 16
KVH = 8
HD = 128
TOP = 2

MESH = pl.DeviceIdType.MESH


def remote(src, dst, send_sem, recv_sem, target):
    return pltpu.make_async_remote_copy(
        src_ref=src,
        dst_ref=dst,
        send_sem=send_sem,
        recv_sem=recv_sem,
        device_id={"blk": target},
        device_id_type=MESH,
    )


def enter(chips, chip, core):
    barrier = pltpu.get_barrier_semaphore()
    pl.semaphore_signal(barrier, inc=1, device_id={"blk": chip * 2 + 1 - core}, device_id_type=MESH)
    for j in range(1, chips):
        other = (chip + j) % chips
        pl.semaphore_signal(barrier, inc=1, device_id={"blk": other * 2 + core}, device_id_type=MESH)
    pl.semaphore_wait(barrier, chips)


def gather_kernel(chips, k_ref, v_ref, ko_ref, vo_ref, send, recv, fsend, frecv, local):
    me = lax.axis_index("blk")
    chip, core = me // 2, me % 2
    sibling = chip * 2 + 1 - core
    pairs = ((k_ref, ko_ref), (v_ref, vo_ref))
    enter(chips, chip, core)
    out = []
    for j in range(1, chips):
        for i, (src, dst) in enumerate(pairs):
            out.append(
                remote(src, dst.at[me], send.at[i, j], recv.at[i, j], (chip + j) % chips * 2 + core)
            )
            out[-1].start()
    for i, (src, dst) in enumerate(pairs):
        out.append(remote(src, dst.at[me], fsend.at[i, 0], frecv.at[i, 0], sibling))
        out[-1].start()
    own = [pltpu.make_async_copy(src, dst.at[me], local.at[i]) for i, (src, dst) in enumerate(pairs)]
    for copy in own:
        copy.start()
    for j in range(1, chips):
        origin = (chip + chips - j) % chips * 2 + core
        for i, (src, dst) in enumerate(pairs):
            remote(src, dst.at[origin], send.at[i, j], recv.at[i, j], sibling).wait_recv()
            out.append(
                remote(dst.at[origin], dst.at[origin], fsend.at[i, j], frecv.at[i, j], sibling)
            )
            out[-1].start()
    for j in range(chips):
        origin = (chip + chips - j) % chips * 2 + 1 - core
        for i, (src, dst) in enumerate(pairs):
            remote(src, dst.at[origin], fsend.at[i, j], frecv.at[i, j], sibling).wait_recv()
    for copy in own:
        copy.wait()
    for copy in out:
        copy.wait_send()


def gather_blocks(keys, values):
    blocks = lax.axis_size("blk")
    chips = blocks // 2
    vmem = pl.BlockSpec(memory_space=pltpu.VMEM)
    shape = jax.ShapeDtypeStruct((blocks,) + keys.shape, keys.dtype)
    dma = pltpu.SemaphoreType.DMA
    k_all, v_all = pl.pallas_call(
        functools.partial(gather_kernel, chips),
        out_shape=(shape, shape),
        in_specs=[vmem, vmem],
        out_specs=(vmem, vmem),
        scratch_shapes=[dma((2, chips)), dma((2, chips)), dma((2, chips)), dma((2, chips)), dma((2,))],
        compiler_params=pltpu.CompilerParams(collective_id=0, has_side_effects=True),
    )(keys, values)
    rows = blocks * keys.shape[0]
    return k_all.reshape(rows, keys.shape[1]), v_all.reshape(rows, keys.shape[1])


def expert_kernel(
    chips,
    tiles,
    x_ref,
    wg_ref,
    wu_ref,
    wd_ref,
    o_ref,
    rows_in,
    acc,
    keep,
    leaving,
    sib_in,
    part_in,
    ag_send,
    ag_recv,
    fw_send,
    fw_recv,
    sib_send,
    sib_recv,
    rs_send,
    rs_recv,
    local,
):
    j, f = pl.program_id(0), pl.program_id(1)
    me = lax.axis_index("blk")
    chip, core = me // 2, me % 2
    sibling = chip * 2 + 1 - core
    rows, width = x_ref.shape
    mid = min(2, tiles - 1)

    def push(k):
        return remote(
            rows_in.at[0, 0], rows_in.at[k, 0], ag_send.at[k], ag_recv.at[k], (chip + k) % chips * 2 + core
        )

    def forward(k):
        return remote(rows_in.at[k, 0], rows_in.at[k, 1], fw_send.at[k], fw_recv.at[k], sibling)

    def exchange(k):
        return remote(leaving.at[k % 2], sib_in.at[k], sib_send.at[k], sib_recv.at[k], sibling)

    def deliver(k):
        return remote(
            sib_in.at[k], part_in.at[k], rs_send.at[k], rs_recv.at[k], (chip + chips - k) % chips * 2 + core
        )

    @pl.when((j == 0) & (f == 0))
    def _():
        own = pltpu.make_async_copy(x_ref, rows_in.at[0, 0], local)
        own.start()
        enter(chips, chip, core)
        own.wait()
        forward(0).start()
        for k in range(1, min(3, chips)):
            push(k).start()

    @pl.when((j >= 1) & (f == 0) & (j + 2 < chips))
    def _():
        push(j + 2).start()

    @pl.when(f == 0)
    def _():
        forward(j).wait_recv()

    tokens = rows_in[j].reshape(2 * rows, width)
    gate = jnp.dot(tokens, wg_ref[...], preferred_element_type=jnp.float32)
    up = jnp.dot(tokens, wu_ref[...], preferred_element_type=jnp.float32)
    hidden = (gate / (1.0 + jnp.exp(-gate)) * up).astype(jnp.bfloat16)
    step = 1024

    @pl.when(f == 0)
    def _():
        for c in range(0, width, step):
            acc[:, c : c + step] = jnp.dot(
                hidden, wd_ref[:, c : c + step], preferred_element_type=jnp.float32
            )

    @pl.when(f > 0)
    def _():
        for c in range(0, width, step):
            acc[:, c : c + step] += jnp.dot(
                hidden, wd_ref[:, c : c + step], preferred_element_type=jnp.float32
            )

    @pl.when((f == mid) & (j + 1 < chips))
    def _():
        push(j + 1).wait_recv()
        forward(j + 1).start()

    def settle(k):
        exchange(k).wait_recv()
        sib_in[k] = (keep[...] + sib_in[k].astype(jnp.float32)).astype(jnp.bfloat16)
        deliver(k).start()

    @pl.when((f == 1) & (j == 1))
    def _():
        exchange(0).wait_recv()
        o_ref[...] += sib_in[0].astype(jnp.float32)

    @pl.when((f == 1) & (j >= 2))
    def _():
        settle(j - 1)

    @pl.when(f == tiles - 1)
    def _():
        @pl.when(j >= 2)
        def _():
            exchange(j - 2).wait_send()

        leaving[j % 2] = acc[rows:, :].astype(jnp.bfloat16)
        exchange(j).start()

        @pl.when(j == 0)
        def _():
            o_ref[...] = acc[:rows, :]

        @pl.when(j > 0)
        def _():
            keep[...] = acc[:rows, :]

        @pl.when(j == chips - 1)
        def _():
            settle(chips - 1)
            for k in range(1, chips):
                deliver(k).wait_recv()
                o_ref[...] += part_in[k].astype(jnp.float32)
            for k in range(chips):
                forward(k).wait_send()
                if k >= 1:
                    push(k).wait_send()
                    deliver(k).wait_send()
            for k in range(max(0, chips - 2), chips):
                exchange(k).wait_send()


def expert_layer(x, gate_w, up_w, down_w):
    blocks = lax.axis_size("blk")
    chips = blocks // 2
    rows, width = x.shape
    units = gate_w.shape[1]
    tile = 256 if units % 256 == 0 else 128
    tiles = units // tile
    dma = pltpu.SemaphoreType.DMA
    low, wide = jnp.bfloat16, jnp.float32
    return pl.pallas_call(
        functools.partial(expert_kernel, chips, tiles),
        grid=(chips, tiles),
        out_shape=jax.ShapeDtypeStruct((rows, width), wide),
        in_specs=[
            pl.BlockSpec(memory_space=pl.ANY),
            pl.BlockSpec((width, tile), lambda j, f: (0, f)),
            pl.BlockSpec((width, tile), lambda j, f: (0, f)),
            pl.BlockSpec((tile, width), lambda j, f: (f, 0)),
        ],
        out_specs=pl.BlockSpec((rows, width), lambda j, f: (0, 0)),
        scratch_shapes=[
            pltpu.VMEM((chips, 2, rows, width), low),
            pltpu.VMEM((2 * rows, width), wide),
            pltpu.VMEM((rows, width), wide),
            pltpu.VMEM((2, rows, width), low),
            pltpu.VMEM((chips, rows, width), low),
            pltpu.VMEM((chips, rows, width), low),
        ]
        + [dma((chips,)) for _ in range(8)]
        + [dma],
        compiler_params=pltpu.CompilerParams(
            collective_id=1,
            has_side_effects=True,
            dimension_semantics=("arbitrary", "arbitrary"),
            vmem_limit_bytes=60 * 1024 * 1024,
        ),
    )(x, gate_w, up_w, down_w)


def on_device(
    residual,
    queries,
    key_cache,
    value_cache,
    segments,
    routes,
    w_out,
    norm_gain,
    w_router,
    w_gate,
    w_up,
    w_down,
):
    tok_rows = queries.shape[0]
    kv_heads = key_cache.shape[1] // HD
    q_per_kv = H // KVH
    seq_block = lax.axis_index("blk")
    head_group = lax.axis_index("expert")
    group_count = lax.axis_size("expert")
    first_row = seq_block * tok_rows
    query_pos = first_row + jnp.arange(tok_rows, dtype=jnp.int32)
    query_seg = lax.dynamic_slice_in_dim(segments, first_row, tok_rows)
    query_four = queries.reshape(tok_rows, kv_heads, q_per_kv, HD)
    score_scale = 1.0 / math.sqrt(HD)
    running = jnp.full((kv_heads, q_per_kv, tok_rows), -1e30, jnp.float32)
    key_rows, value_rows = gather_blocks(key_cache, value_cache)
    piece_len = key_rows.shape[0]
    key_pos = jnp.arange(piece_len, dtype=jnp.int32)
    visible = (query_seg[:, None] == segments[None, :]) & (key_pos[None, :] <= query_pos[:, None])
    scores = (
        jnp.einsum(
            "qkgd,skd->kgqs",
            query_four,
            key_rows.reshape(piece_len, kv_heads, HD),
            preferred_element_type=jnp.float32,
        )
        * score_scale
    )
    scores = jnp.where(visible, scores, -1e30)
    newmax = jnp.maximum(running, jnp.max(scores, axis=-1))
    weights = jnp.where(visible, jnp.exp(scores - newmax[..., None]), 0.0)
    totals = jnp.sum(weights, axis=-1)
    weighted_sum = jnp.einsum(
        "kgqs,skd->kgqd",
        weights.astype(jnp.bfloat16),
        value_rows.reshape(piece_len, kv_heads, HD),
        preferred_element_type=jnp.float32,
    )
    running, totals, weighted_sum = (newmax, totals, weighted_sum)
    attended = (
        jnp.transpose(weighted_sum / totals[..., None], (2, 0, 1, 3))
        .reshape(tok_rows, kv_heads * q_per_kv * HD)
        .astype(jnp.bfloat16)
    )
    head_term = jnp.dot(attended, w_out, preferred_element_type=jnp.float32)
    feat_width = residual.shape[1]
    own_cols = lax.dynamic_slice_in_dim(
        head_term, head_group * feat_width, feat_width, 1
    ) + residual.astype(jnp.float32)
    head_term = lax.dynamic_update_slice_in_dim(head_term, own_cols, head_group * feat_width, 1)
    row_share = tok_rows // group_count
    summed = lax.psum(head_term.astype(jnp.bfloat16), "expert").astype(jnp.float32)
    normed = (
        summed * lax.rsqrt(jnp.mean(summed * summed, axis=-1, keepdims=True) + 1e-05) * norm_gain
    ).astype(jnp.bfloat16)
    own_rows = lax.dynamic_slice_in_dim(summed, head_group * row_share, row_share, 0)
    gate_score = jax.nn.sigmoid(jnp.dot(normed, w_router, preferred_element_type=jnp.float32))
    picked = routes[:, :, None] == jnp.arange(w_router.shape[1], dtype=jnp.int32)[None, None, :]
    chosen = jnp.sum(jnp.where(picked, gate_score[:, None, :], 0.0), axis=-1)
    mixing = chosen / jnp.sum(chosen, axis=-1, keepdims=True)
    expert_id = head_group * w_gate.shape[0]
    chosen_here = routes == expert_id
    routed = jnp.any(chosen_here, axis=-1)
    share_w = jnp.sum(jnp.where(chosen_here, mixing, 0.0), axis=-1)
    capacity = tok_rows * TOP * 9 // (8 * w_gate.shape[0] * group_count)
    capacity = -(-capacity // 16) * 16
    slot_index = jnp.cumsum(routed.astype(jnp.int32)) - 1
    placing = (
        (slot_index[None, :] == jnp.arange(capacity, dtype=jnp.int32)[:, None]) & routed[None, :]
    ).astype(jnp.bfloat16)
    buffer = jnp.dot(placing, normed, preferred_element_type=jnp.float32).astype(jnp.bfloat16)
    gate_w = w_gate[0]
    up_w = w_up[0]
    down_w = w_down[0]
    expert_out = expert_layer(buffer, gate_w, up_w, down_w)
    contrib = jnp.take(expert_out, jnp.clip(slot_index, 0, capacity - 1), axis=0) * share_w[:, None]
    combined = lax.psum_scatter(
        contrib.astype(jnp.bfloat16), "expert", scatter_dimension=0, tiled=True
    ).astype(jnp.float32)
    return (own_rows + combined).astype(jnp.bfloat16)


def solution(mesh):
    return jax.shard_map(
        on_device,
        mesh=mesh,
        in_specs=(
            P("blk", "expert"),
            P("blk", "expert"),
            P("blk", "expert"),
            P("blk", "expert"),
            P(),
            P("blk", None),
            P("expert", None),
            P(),
            P(),
            P("expert", None, "blk"),
            P("expert", None, "blk"),
            P("expert", "blk", None),
        ),
        out_specs=P(("blk", "expert"), None),
        check_vma=False,
    )
```

```python
import functools
import math

import jax
import jax.numpy as jnp
from jax import lax
from jax.experimental import pallas as pl
from jax.experimental.pallas import tpu as pltpu
from jax.sharding import PartitionSpec as P

H = 16
KVH = 8
HD = 128
TOP = 2

MESH = pl.DeviceIdType.MESH


def remote(src, dst, send_sem, recv_sem, target, axis="blk"):
    return pltpu.make_async_remote_copy(
        src_ref=src,
        dst_ref=dst,
        send_sem=send_sem,
        recv_sem=recv_sem,
        device_id={axis: target},
        device_id_type=MESH,
    )


def enter(chips, chip, core, experts=1):
    barrier = pltpu.get_barrier_semaphore()
    if chips > 0:
        pl.semaphore_signal(
            barrier, inc=1, device_id={"blk": chip * 2 + 1 - core}, device_id_type=MESH
        )
    for j in range(1, chips):
        other = (chip + j) % chips
        pl.semaphore_signal(barrier, inc=1, device_id={"blk": other * 2 + core}, device_id_type=MESH)
    for k in range(1, experts):
        other = (lax.axis_index("expert") + k) % experts
        pl.semaphore_signal(barrier, inc=1, device_id={"expert": other}, device_id_type=MESH)
    pl.semaphore_wait(barrier, chips + experts - 1)


def gather_kernel(
    chips, experts, k_ref, v_ref, w_ref, ko_ref, vo_ref, wo_ref,
    send, recv, fsend, frecv, local, wsend, wrecv,
):
    me = lax.axis_index("blk")
    chip, core = me // 2, me % 2
    sibling = chip * 2 + 1 - core
    pairs = ((k_ref, ko_ref), (v_ref, vo_ref))
    group = lax.axis_index("expert")
    enter(chips, chip, core, experts)
    out = []
    part, cols = wo_ref.shape[1], wo_ref.shape[2]
    mine = pl.ds(pl.multiple_of(me * part, part), part)

    def piece(k):
        target = (group + k) % experts
        return w_ref.at[mine, pl.ds(pl.multiple_of(target * cols, 128), cols)]

    def lend(k):
        return remote(
            piece(k), wo_ref.at[group], wsend.at[k], wrecv.at[k], (group + k) % experts, "expert"
        )

    for k in range(1, experts):
        lend(k).start()
    for j in range(1, chips):
        for i, (src, dst) in enumerate(pairs):
            out.append(
                remote(src, dst.at[me], send.at[i, j], recv.at[i, j], (chip + j) % chips * 2 + core)
            )
            out[-1].start()
    for i, (src, dst) in enumerate(pairs):
        out.append(remote(src, dst.at[me], fsend.at[i, 0], frecv.at[i, 0], sibling))
        out[-1].start()
    own = [pltpu.make_async_copy(src, dst.at[me], local.at[i]) for i, (src, dst) in enumerate(pairs)]
    own.append(pltpu.make_async_copy(piece(0), wo_ref.at[group], local.at[2]))
    for copy in own:
        copy.start()
    for j in range(1, chips):
        origin = (chip + chips - j) % chips * 2 + core
        for i, (src, dst) in enumerate(pairs):
            remote(src, dst.at[origin], send.at[i, j], recv.at[i, j], sibling).wait_recv()
            out.append(
                remote(dst.at[origin], dst.at[origin], fsend.at[i, j], frecv.at[i, j], sibling)
            )
            out[-1].start()
    for j in range(chips):
        origin = (chip + chips - j) % chips * 2 + 1 - core
        for i, (src, dst) in enumerate(pairs):
            remote(src, dst.at[origin], fsend.at[i, j], frecv.at[i, j], sibling).wait_recv()
    for copy in own:
        copy.wait()
    for k in range(1, experts):
        origin = (group + experts - k) % experts
        remote(
            piece(k), wo_ref.at[origin], wsend.at[k], wrecv.at[k], (group + k) % experts, "expert"
        ).wait_recv()
        lend(k).wait_send()
    for copy in out:
        copy.wait_send()


def gather_blocks(keys, values, w_out):
    blocks, experts = lax.axis_size("blk"), lax.axis_size("expert")
    chips = blocks // 2
    vmem = pl.BlockSpec(memory_space=pltpu.VMEM)
    shape = jax.ShapeDtypeStruct((blocks,) + keys.shape, keys.dtype)
    wshape = jax.ShapeDtypeStruct(
        (experts, w_out.shape[0] // blocks, w_out.shape[1] // experts), w_out.dtype
    )
    dma = pltpu.SemaphoreType.DMA
    k_all, v_all, w_part = pl.pallas_call(
        functools.partial(gather_kernel, chips, experts),
        out_shape=(shape, shape, wshape),
        in_specs=[vmem, vmem, pl.BlockSpec(memory_space=pl.ANY)],
        out_specs=(vmem, vmem, vmem),
        scratch_shapes=[dma((2, chips)), dma((2, chips)), dma((2, chips)), dma((2, chips)), dma((3,))]
        + [dma((experts,)), dma((experts,))],
        compiler_params=pltpu.CompilerParams(collective_id=0, has_side_effects=True),
    )(keys, values, w_out)
    rows = blocks * keys.shape[0]
    return k_all.reshape(rows, keys.shape[1]), v_all.reshape(rows, keys.shape[1]), w_part


def heads_kernel(experts, x_ref, o_ref, send, recv, local):
    group = lax.axis_index("expert")
    cols = x_ref.shape[1]

    def place(g):
        return o_ref.at[:, pl.ds(pl.multiple_of(g * cols, 128), cols)]

    def push(k, slot):
        return remote(
            x_ref, place(slot), send.at[k], recv.at[k], (group + k) % experts, "expert"
        )

    enter(0, 0, 0, experts)
    for k in range(experts - 1, 0, -1):
        push(k, group).start()
    own = pltpu.make_async_copy(x_ref, place(group), local)
    own.start()
    own.wait()
    for k in range(1, experts):
        push(k, (group + experts - k) % experts).wait_recv()
        push(k, group).wait_send()


def gather_heads(attended):
    experts = lax.axis_size("expert")
    vmem = pl.BlockSpec(memory_space=pltpu.VMEM)
    dma = pltpu.SemaphoreType.DMA
    rows, cols = attended.shape
    return pl.pallas_call(
        functools.partial(heads_kernel, experts),
        out_shape=jax.ShapeDtypeStruct((rows, cols * experts), attended.dtype),
        in_specs=[vmem],
        out_specs=vmem,
        scratch_shapes=[dma((experts,)), dma((experts,)), dma],
        compiler_params=pltpu.CompilerParams(collective_id=2, has_side_effects=True),
    )(attended)


def mix_kernel(
    experts, att_ref, w_ref, res_ref, gain_ref, router_ref, place_ref, stream_ref, buf_ref, logit_ref,
    squares, logits, chosen, s_send, s_recv, l_send, l_recv, d_send, d_recv,
):
    group = lax.axis_index("expert")
    rows, cols = res_ref.shape

    def target(k):
        return (group + k) % experts

    def share_squares(k):
        return remote(
            squares.at[0], squares.at[k], s_send.at[k], s_recv.at[k], target(k), "expert"
        )

    def share_logits(k):
        return remote(logits.at[0], logits.at[k], l_send.at[k], l_recv.at[k], target(k), "expert")

    def slot(g):
        return pl.ds(pl.multiple_of(g * cols, 128), cols)

    def dispatch(k, g):
        return remote(
            chosen.at[k], buf_ref.at[:, slot(g)], d_send.at[k], d_recv.at[k], target(k), "expert"
        )

    stream = res_ref[...].astype(jnp.float32) + jnp.dot(
        att_ref[...], w_ref[...], preferred_element_type=jnp.float32
    )
    stream_ref[...] = stream
    total = jnp.sum(stream * stream, axis=-1, keepdims=True)
    squares[0] = jnp.transpose(jnp.broadcast_to(total, (rows, 128)))[:8, :]
    enter(0, 0, 0, experts)
    for k in range(1, experts):
        share_squares(k).start()
    for k in range(1, experts):
        share_squares(k).wait_recv()
    total = squares[0]
    for k in range(1, experts):
        total = total + squares[k]
    total = jnp.transpose(jnp.broadcast_to(total[:1, :], (128, rows)))[:, :1]
    scale = lax.rsqrt(total * (1.0 / (cols * experts)) + 1e-05)
    normed = (stream_ref[...] * scale * gain_ref[...]).astype(jnp.bfloat16)
    for k in range(experts - 1, 0, -1):
        chosen[k] = jnp.dot(
            place_ref[target(k)], normed, preferred_element_type=jnp.float32
        ).astype(jnp.bfloat16)
        dispatch(k, group).start()
    logits[0] = lax.dot_general(
        router_ref[...], normed, (((1,), (1,)), ((), ())), preferred_element_type=jnp.float32
    )
    for k in range(1, experts):
        share_logits(k).start()
    buf_ref[:, slot(group)] = jnp.dot(
        place_ref[group], normed, preferred_element_type=jnp.float32
    ).astype(jnp.bfloat16)
    for k in range(1, experts):
        share_logits(k).wait_recv()
    total = logits[0]
    for k in range(1, experts):
        total = total + logits[k]
    logit_ref[...] = total
    for k in range(1, experts):
        dispatch(k, target(experts - k)).wait_recv()
    for k in range(1, experts):
        share_squares(k).wait_send()
        share_logits(k).wait_send()
        dispatch(k, group).wait_send()


def mix_columns(attended, w_cols, residual, gain, router, placing):
    experts = lax.axis_size("expert")
    rows, cols = residual.shape
    capacity = placing.shape[1]
    vmem = pl.BlockSpec(memory_space=pltpu.VMEM)
    dma = pltpu.SemaphoreType.DMA
    shape = jax.ShapeDtypeStruct
    return pl.pallas_call(
        functools.partial(mix_kernel, experts),
        out_shape=(
            shape((rows, cols), jnp.float32),
            shape((capacity, cols * experts), jnp.bfloat16),
            shape((router.shape[0], rows), jnp.float32),
        ),
        in_specs=[vmem] * 6,
        out_specs=(vmem, vmem, vmem),
        scratch_shapes=[
            pltpu.VMEM((experts, 8, rows), jnp.float32),
            pltpu.VMEM((experts, router.shape[0], rows), jnp.float32),
            pltpu.VMEM((experts, capacity, cols), jnp.bfloat16),
        ]
        + [dma((experts,)) for _ in range(6)],
        compiler_params=pltpu.CompilerParams(
            collective_id=3, has_side_effects=True, vmem_limit_bytes=40 * 1024 * 1024
        ),
    )(attended, w_cols, residual, gain, router, placing)


def combine_kernel(
    experts, eo_ref, stream_ref, place_ref, share_ref, o_ref,
    low, arrived, final, e_send, e_recv, f_send, f_recv, local,
):
    group = lax.axis_index("expert")
    rows, cols = stream_ref.shape
    own_rows = rows // experts

    def target(k):
        return (group + k) % experts

    def slot(g):
        return pl.ds(pl.multiple_of(g * cols, 128), cols)

    def strip(g):
        return pl.ds(pl.multiple_of(g * own_rows, own_rows), own_rows)

    def give(k, g):
        return remote(
            low.at[:, slot(target(k))], arrived.at[g], e_send.at[k], e_recv.at[k], target(k), "expert"
        )

    def finish(k, g):
        return remote(
            final.at[strip(target(k)), :], o_ref.at[:, slot(g)], f_send.at[k], f_recv.at[k],
            target(k), "expert",
        )

    low[...] = eo_ref[...].astype(jnp.bfloat16)
    enter(0, 0, 0, experts)
    for k in range(experts - 1, 0, -1):
        give(k, group).start()
    own = pltpu.make_async_copy(low.at[:, slot(group)], arrived.at[group], local.at[0])
    own.start()
    own.wait()
    for k in range(1, experts):
        give(k, target(experts - k)).wait_recv()
    total = stream_ref[...]
    for g in range(experts):
        total = total + share_ref[:, g : g + 1] * jnp.dot(
            place_ref[g], arrived[g], preferred_element_type=jnp.float32
        )
    final[...] = total.astype(jnp.bfloat16)
    for k in range(experts - 1, 0, -1):
        finish(k, group).start()
    own = pltpu.make_async_copy(final.at[strip(group), :], o_ref.at[:, slot(group)], local.at[1])
    own.start()
    own.wait()
    for k in range(1, experts):
        finish(k, target(experts - k)).wait_recv()
    for k in range(1, experts):
        give(k, group).wait_send()
        finish(k, group).wait_send()


def combine(expert_out, stream, placing, shares):
    experts = lax.axis_size("expert")
    rows, cols = stream.shape
    capacity = expert_out.shape[0]
    vmem = pl.BlockSpec(memory_space=pltpu.VMEM)
    dma = pltpu.SemaphoreType.DMA
    return pl.pallas_call(
        functools.partial(combine_kernel, experts),
        out_shape=jax.ShapeDtypeStruct((rows // experts, cols * experts), jnp.bfloat16),
        in_specs=[vmem] * 4,
        out_specs=vmem,
        scratch_shapes=[
            pltpu.VMEM((capacity, cols * experts), jnp.bfloat16),
            pltpu.VMEM((experts, capacity, cols), jnp.bfloat16),
            pltpu.VMEM((rows, cols), jnp.bfloat16),
        ]
        + [dma((experts,)) for _ in range(4)]
        + [dma((2,))],
        compiler_params=pltpu.CompilerParams(
            collective_id=4, has_side_effects=True, vmem_limit_bytes=40 * 1024 * 1024
        ),
    )(expert_out, stream, placing, shares)


def expert_kernel(
    chips,
    tiles,
    x_ref,
    wg_ref,
    wu_ref,
    wd_ref,
    o_ref,
    rows_in,
    acc,
    keep,
    leaving,
    sib_in,
    part_in,
    ag_send,
    ag_recv,
    fw_send,
    fw_recv,
    sib_send,
    sib_recv,
    rs_send,
    rs_recv,
    local,
):
    j, f = pl.program_id(0), pl.program_id(1)
    me = lax.axis_index("blk")
    chip, core = me // 2, me % 2
    sibling = chip * 2 + 1 - core
    rows, width = x_ref.shape
    mid = min(2, tiles - 1)

    def push(k):
        return remote(
            rows_in.at[0, 0], rows_in.at[k, 0], ag_send.at[k], ag_recv.at[k], (chip + k) % chips * 2 + core
        )

    def forward(k):
        return remote(rows_in.at[k, 0], rows_in.at[k, 1], fw_send.at[k], fw_recv.at[k], sibling)

    def exchange(k):
        return remote(leaving.at[k % 2], sib_in.at[k], sib_send.at[k], sib_recv.at[k], sibling)

    def deliver(k):
        return remote(
            sib_in.at[k], part_in.at[k], rs_send.at[k], rs_recv.at[k], (chip + chips - k) % chips * 2 + core
        )

    @pl.when((j == 0) & (f == 0))
    def _():
        own = pltpu.make_async_copy(x_ref, rows_in.at[0, 0], local)
        own.start()
        enter(chips, chip, core)
        own.wait()
        forward(0).start()
        for k in range(1, min(3, chips)):
            push(k).start()

    @pl.when((j >= 1) & (f == 0) & (j + 2 < chips))
    def _():
        push(j + 2).start()

    @pl.when(f == 0)
    def _():
        forward(j).wait_recv()

    tokens = rows_in[j].reshape(2 * rows, width)
    gate = jnp.dot(tokens, wg_ref[...], preferred_element_type=jnp.float32)
    up = jnp.dot(tokens, wu_ref[...], preferred_element_type=jnp.float32)
    hidden = (gate / (1.0 + jnp.exp(-gate)) * up).astype(jnp.bfloat16)
    step = 1024

    @pl.when(f == 0)
    def _():
        for c in range(0, width, step):
            acc[:, c : c + step] = jnp.dot(
                hidden, wd_ref[:, c : c + step], preferred_element_type=jnp.float32
            )

    @pl.when(f > 0)
    def _():
        for c in range(0, width, step):
            acc[:, c : c + step] += jnp.dot(
                hidden, wd_ref[:, c : c + step], preferred_element_type=jnp.float32
            )

    @pl.when((f == mid) & (j + 1 < chips))
    def _():
        push(j + 1).wait_recv()
        forward(j + 1).start()

    def settle(k):
        exchange(k).wait_recv()
        sib_in[k] = (keep[...] + sib_in[k].astype(jnp.float32)).astype(jnp.bfloat16)
        deliver(k).start()

    @pl.when((f == 1) & (j == 1))
    def _():
        exchange(0).wait_recv()
        o_ref[...] += sib_in[0].astype(jnp.float32)

    @pl.when((f == 1) & (j >= 2))
    def _():
        settle(j - 1)

    @pl.when(f == tiles - 1)
    def _():
        @pl.when(j >= 2)
        def _():
            exchange(j - 2).wait_send()

        leaving[j % 2] = acc[rows:, :].astype(jnp.bfloat16)
        exchange(j).start()

        @pl.when(j == 0)
        def _():
            o_ref[...] = acc[:rows, :]

        @pl.when(j > 0)
        def _():
            keep[...] = acc[:rows, :]

        @pl.when(j == chips - 1)
        def _():
            settle(chips - 1)
            for k in range(1, chips):
                deliver(k).wait_recv()
                o_ref[...] += part_in[k].astype(jnp.float32)
            for k in range(chips):
                forward(k).wait_send()
                if k >= 1:
                    push(k).wait_send()
                    deliver(k).wait_send()
            for k in range(max(0, chips - 2), chips):
                exchange(k).wait_send()


def expert_layer(x, gate_w, up_w, down_w):
    blocks = lax.axis_size("blk")
    chips = blocks // 2
    rows, width = x.shape
    units = gate_w.shape[1]
    tile = 256 if units % 256 == 0 else 128
    tiles = units // tile
    dma = pltpu.SemaphoreType.DMA
    low, wide = jnp.bfloat16, jnp.float32
    return pl.pallas_call(
        functools.partial(expert_kernel, chips, tiles),
        grid=(chips, tiles),
        out_shape=jax.ShapeDtypeStruct((rows, width), wide),
        in_specs=[
            pl.BlockSpec(memory_space=pl.ANY),
            pl.BlockSpec((width, tile), lambda j, f: (0, f)),
            pl.BlockSpec((width, tile), lambda j, f: (0, f)),
            pl.BlockSpec((tile, width), lambda j, f: (f, 0)),
        ],
        out_specs=pl.BlockSpec((rows, width), lambda j, f: (0, 0)),
        scratch_shapes=[
            pltpu.VMEM((chips, 2, rows, width), low),
            pltpu.VMEM((2 * rows, width), wide),
            pltpu.VMEM((rows, width), wide),
            pltpu.VMEM((2, rows, width), low),
            pltpu.VMEM((chips, rows, width), low),
            pltpu.VMEM((chips, rows, width), low),
        ]
        + [dma((chips,)) for _ in range(8)]
        + [dma],
        compiler_params=pltpu.CompilerParams(
            collective_id=1,
            has_side_effects=True,
            dimension_semantics=("arbitrary", "arbitrary"),
            vmem_limit_bytes=60 * 1024 * 1024,
        ),
    )(x, gate_w, up_w, down_w)


def on_device(
    residual,
    queries,
    key_cache,
    value_cache,
    segments,
    routes,
    w_out,
    norm_gain,
    w_router,
    w_gate,
    w_up,
    w_down,
):
    tok_rows = queries.shape[0]
    kv_heads = key_cache.shape[1] // HD
    q_per_kv = H // KVH
    seq_block = lax.axis_index("blk")
    head_group = lax.axis_index("expert")
    first_row = seq_block * tok_rows
    query_pos = first_row + jnp.arange(tok_rows, dtype=jnp.int32)
    query_seg = lax.dynamic_slice_in_dim(segments, first_row, tok_rows)
    query_four = queries.reshape(tok_rows, kv_heads, q_per_kv, HD)
    score_scale = 1.0 / math.sqrt(HD)
    running = jnp.full((kv_heads, q_per_kv, tok_rows), -1e30, jnp.float32)
    key_rows, value_rows, w_part = gather_blocks(key_cache, value_cache, w_out)
    w_cols = lax.all_gather(w_part, "blk", axis=1, tiled=True)
    w_cols = w_cols.reshape(-1, w_cols.shape[2])
    piece_len = key_rows.shape[0]
    key_pos = jnp.arange(piece_len, dtype=jnp.int32)
    visible = (query_seg[:, None] == segments[None, :]) & (key_pos[None, :] <= query_pos[:, None])
    scores = (
        jnp.einsum(
            "qkgd,skd->kgqs",
            query_four,
            key_rows.reshape(piece_len, kv_heads, HD),
            preferred_element_type=jnp.float32,
        )
        * score_scale
    )
    scores = jnp.where(visible, scores, -1e30)
    newmax = jnp.maximum(running, jnp.max(scores, axis=-1))
    weights = jnp.where(visible, jnp.exp(scores - newmax[..., None]), 0.0)
    totals = jnp.sum(weights, axis=-1)
    weighted_sum = jnp.einsum(
        "kgqs,skd->kgqd",
        weights.astype(jnp.bfloat16),
        value_rows.reshape(piece_len, kv_heads, HD),
        preferred_element_type=jnp.float32,
    )
    running, totals, weighted_sum = (newmax, totals, weighted_sum)
    attended = (
        jnp.transpose(weighted_sum / totals[..., None], (2, 0, 1, 3))
        .reshape(tok_rows, kv_heads * q_per_kv * HD)
        .astype(jnp.bfloat16)
    )
    feat_width = residual.shape[1]
    experts = w_router.shape[1]
    first_col = head_group * feat_width
    capacity = tok_rows * TOP * 9 // (8 * experts)
    capacity = -(-capacity // 16) * 16
    ids = jnp.arange(experts, dtype=jnp.int32)
    picked = routes[:, :, None] == ids[None, None, :]
    routed = jnp.any(picked, axis=1).T
    slot_index = jnp.where(routed, jnp.cumsum(routed.astype(jnp.int32), axis=1) - 1, -1)
    slots = jnp.arange(capacity, dtype=jnp.int32)
    placing = (slot_index[:, None, :] == slots[None, :, None]).astype(jnp.bfloat16)
    placing_back = (slot_index[:, :, None] == slots[None, None, :]).astype(jnp.bfloat16)
    router = lax.dynamic_slice_in_dim(w_router, first_col, feat_width, 0).T
    router = jnp.pad(router, ((0, -experts % 16), (0, 0)))
    gain = lax.dynamic_slice_in_dim(norm_gain, first_col, feat_width)[None, :]
    attended = gather_heads(attended)
    stream, buffer, logits = mix_columns(attended, w_cols, residual, gain, router, placing)
    gate_score = jax.nn.sigmoid(logits[:experts, :].T)
    chosen = jnp.where(routed.T, gate_score, 0.0)
    shares = chosen / jnp.sum(chosen, axis=-1, keepdims=True)
    shares = jnp.pad(shares, ((0, 0), (0, -experts % 128)))
    expert_out = expert_layer(buffer, w_gate[0], w_up[0], w_down[0])
    return combine(expert_out, stream, placing_back, shares)


def solution(mesh):
    return jax.shard_map(
        on_device,
        mesh=mesh,
        in_specs=(
            P("blk", "expert"),
            P("blk", "expert"),
            P("blk", "expert"),
            P("blk", "expert"),
            P(),
            P("blk", None),
            P("expert", None),
            P(),
            P(),
            P("expert", None, "blk"),
            P("expert", None, "blk"),
            P("expert", "blk", None),
        ),
        out_specs=P(("blk", "expert"), None),
        check_vma=False,
    )
```

```python
import functools
import math

import jax
import jax.numpy as jnp
from jax import lax
from jax.experimental import pallas as pl
from jax.experimental.pallas import tpu as pltpu
from jax.sharding import PartitionSpec as P

H = 16
KVH = 8
HD = 128
TOP = 2

MESH = pl.DeviceIdType.MESH


def remote(src, dst, send_sem, recv_sem, target, axis="blk"):
    return pltpu.make_async_remote_copy(
        src_ref=src,
        dst_ref=dst,
        send_sem=send_sem,
        recv_sem=recv_sem,
        device_id={axis: target},
        device_id_type=MESH,
    )


def enter(chips, chip, core, experts=1):
    barrier = pltpu.get_barrier_semaphore()
    if chips > 0:
        pl.semaphore_signal(
            barrier, inc=1, device_id={"blk": chip * 2 + 1 - core}, device_id_type=MESH
        )
    for j in range(1, chips):
        other = (chip + j) % chips
        pl.semaphore_signal(barrier, inc=1, device_id={"blk": other * 2 + core}, device_id_type=MESH)
    for k in range(1, experts):
        other = (lax.axis_index("expert") + k) % experts
        pl.semaphore_signal(barrier, inc=1, device_id={"expert": other}, device_id_type=MESH)
    pl.semaphore_wait(barrier, chips + experts - 1)


def gather_kernel(
    chips, experts, k_ref, v_ref, w_ref, ko_ref, vo_ref, wo_ref,
    send, recv, fsend, frecv, local, wsend, wrecv,
):
    me = lax.axis_index("blk")
    chip, core = me // 2, me % 2
    sibling = chip * 2 + 1 - core
    pairs = ((k_ref, ko_ref), (v_ref, vo_ref))
    group = lax.axis_index("expert")
    enter(chips, chip, core, experts)
    out = []
    part, cols = wo_ref.shape[1], wo_ref.shape[2]
    mine = pl.ds(pl.multiple_of(me * part, part), part)

    def piece(k):
        target = (group + k) % experts
        return w_ref.at[mine, pl.ds(pl.multiple_of(target * cols, 128), cols)]

    def lend(k):
        return remote(
            piece(k), wo_ref.at[group], wsend.at[k], wrecv.at[k], (group + k) % experts, "expert"
        )

    for k in range(1, experts):
        lend(k).start()
    for j in range(1, chips):
        for i, (src, dst) in enumerate(pairs):
            out.append(
                remote(src, dst.at[me], send.at[i, j], recv.at[i, j], (chip + j) % chips * 2 + core)
            )
            out[-1].start()
    for i, (src, dst) in enumerate(pairs):
        out.append(remote(src, dst.at[me], fsend.at[i, 0], frecv.at[i, 0], sibling))
        out[-1].start()
    own = [pltpu.make_async_copy(src, dst.at[me], local.at[i]) for i, (src, dst) in enumerate(pairs)]
    own.append(pltpu.make_async_copy(piece(0), wo_ref.at[group], local.at[2]))
    for copy in own:
        copy.start()
    for j in range(1, chips):
        origin = (chip + chips - j) % chips * 2 + core
        for i, (src, dst) in enumerate(pairs):
            remote(src, dst.at[origin], send.at[i, j], recv.at[i, j], sibling).wait_recv()
            out.append(
                remote(dst.at[origin], dst.at[origin], fsend.at[i, j], frecv.at[i, j], sibling)
            )
            out[-1].start()
    for j in range(chips):
        origin = (chip + chips - j) % chips * 2 + 1 - core
        for i, (src, dst) in enumerate(pairs):
            remote(src, dst.at[origin], fsend.at[i, j], frecv.at[i, j], sibling).wait_recv()
    for copy in own:
        copy.wait()
    for k in range(1, experts):
        origin = (group + experts - k) % experts
        remote(
            piece(k), wo_ref.at[origin], wsend.at[k], wrecv.at[k], (group + k) % experts, "expert"
        ).wait_recv()
        lend(k).wait_send()
    for copy in out:
        copy.wait_send()


def gather_blocks(keys, values, w_out):
    blocks, experts = lax.axis_size("blk"), lax.axis_size("expert")
    chips = blocks // 2
    vmem = pl.BlockSpec(memory_space=pltpu.VMEM)
    shape = jax.ShapeDtypeStruct((blocks,) + keys.shape, keys.dtype)
    wshape = jax.ShapeDtypeStruct(
        (experts, w_out.shape[0] // blocks, w_out.shape[1] // experts), w_out.dtype
    )
    dma = pltpu.SemaphoreType.DMA
    k_all, v_all, w_part = pl.pallas_call(
        functools.partial(gather_kernel, chips, experts),
        out_shape=(shape, shape, wshape),
        in_specs=[vmem, vmem, pl.BlockSpec(memory_space=pl.ANY)],
        out_specs=(vmem, vmem, vmem),
        scratch_shapes=[dma((2, chips)), dma((2, chips)), dma((2, chips)), dma((2, chips)), dma((3,))]
        + [dma((experts,)), dma((experts,))],
        compiler_params=pltpu.CompilerParams(collective_id=0, has_side_effects=True),
    )(keys, values, w_out)
    rows = blocks * keys.shape[0]
    return k_all.reshape(rows, keys.shape[1]), v_all.reshape(rows, keys.shape[1]), w_part


def heads_kernel(experts, x_ref, o_ref, send, recv, local):
    group = lax.axis_index("expert")
    cols = x_ref.shape[1]

    def place(g):
        return o_ref.at[:, pl.ds(pl.multiple_of(g * cols, 128), cols)]

    def push(k, slot):
        return remote(
            x_ref, place(slot), send.at[k], recv.at[k], (group + k) % experts, "expert"
        )

    enter(0, 0, 0, experts)
    for k in range(experts - 1, 0, -1):
        push(k, group).start()
    own = pltpu.make_async_copy(x_ref, place(group), local)
    own.start()
    own.wait()
    for k in range(1, experts):
        push(k, (group + experts - k) % experts).wait_recv()
        push(k, group).wait_send()


def gather_heads(attended):
    experts = lax.axis_size("expert")
    vmem = pl.BlockSpec(memory_space=pltpu.VMEM)
    dma = pltpu.SemaphoreType.DMA
    rows, cols = attended.shape
    return pl.pallas_call(
        functools.partial(heads_kernel, experts),
        out_shape=jax.ShapeDtypeStruct((rows, cols * experts), attended.dtype),
        in_specs=[vmem],
        out_specs=vmem,
        scratch_shapes=[dma((experts,)), dma((experts,)), dma],
        compiler_params=pltpu.CompilerParams(collective_id=2, has_side_effects=True),
    )(attended)


def mix_kernel(
    experts, att_ref, w_ref, res_ref, gain_ref, router_ref, place_ref, stream_ref, buf_ref, logit_ref,
    squares, logits, chosen, s_send, s_recv, l_send, l_recv, d_send, d_recv,
):
    group = lax.axis_index("expert")
    rows, cols = res_ref.shape

    def target(k):
        return (group + k) % experts

    def share_squares(k):
        return remote(
            squares.at[0], squares.at[k], s_send.at[k], s_recv.at[k], target(k), "expert"
        )

    def share_logits(k):
        return remote(logits.at[0], logits.at[k], l_send.at[k], l_recv.at[k], target(k), "expert")

    def slot(g):
        return pl.ds(pl.multiple_of(g * cols, 128), cols)

    def dispatch(k, g):
        return remote(
            chosen.at[k], buf_ref.at[:, slot(g)], d_send.at[k], d_recv.at[k], target(k), "expert"
        )

    stream = res_ref[...].astype(jnp.float32) + jnp.dot(
        att_ref[...], w_ref[...], preferred_element_type=jnp.float32
    )
    stream_ref[...] = stream
    total = jnp.sum(stream * stream, axis=-1, keepdims=True)
    squares[0] = jnp.transpose(jnp.broadcast_to(total, (rows, 128)))[:8, :]
    enter(0, 0, 0, experts)
    for k in range(1, experts):
        share_squares(k).start()
    for k in range(1, experts):
        share_squares(k).wait_recv()
    total = squares[0]
    for k in range(1, experts):
        total = total + squares[k]
    total = jnp.transpose(jnp.broadcast_to(total[:1, :], (128, rows)))[:, :1]
    scale = lax.rsqrt(total * (1.0 / (cols * experts)) + 1e-05)
    normed = (stream_ref[...] * scale * gain_ref[...]).astype(jnp.bfloat16)
    for k in range(experts - 1, 0, -1):
        chosen[k] = jnp.dot(
            place_ref[target(k)], normed, preferred_element_type=jnp.float32
        ).astype(jnp.bfloat16)
        dispatch(k, group).start()
    logits[0] = lax.dot_general(
        router_ref[...], normed, (((1,), (1,)), ((), ())), preferred_element_type=jnp.float32
    )
    for k in range(1, experts):
        share_logits(k).start()
    buf_ref[:, slot(group)] = jnp.dot(
        place_ref[group], normed, preferred_element_type=jnp.float32
    ).astype(jnp.bfloat16)
    for k in range(1, experts):
        share_logits(k).wait_recv()
    total = logits[0]
    for k in range(1, experts):
        total = total + logits[k]
    logit_ref[...] = total
    for k in range(1, experts):
        dispatch(k, target(experts - k)).wait_recv()
    for k in range(1, experts):
        share_squares(k).wait_send()
        share_logits(k).wait_send()
        dispatch(k, group).wait_send()


def mix_columns(attended, w_cols, residual, gain, router, placing):
    experts = lax.axis_size("expert")
    rows, cols = residual.shape
    capacity = placing.shape[1]
    vmem = pl.BlockSpec(memory_space=pltpu.VMEM)
    dma = pltpu.SemaphoreType.DMA
    shape = jax.ShapeDtypeStruct
    return pl.pallas_call(
        functools.partial(mix_kernel, experts),
        out_shape=(
            shape((rows, cols), jnp.float32),
            shape((capacity, cols * experts), jnp.bfloat16),
            shape((router.shape[0], rows), jnp.float32),
        ),
        in_specs=[vmem] * 6,
        out_specs=(vmem, vmem, vmem),
        scratch_shapes=[
            pltpu.VMEM((experts, 8, rows), jnp.float32),
            pltpu.VMEM((experts, router.shape[0], rows), jnp.float32),
            pltpu.VMEM((experts, capacity, cols), jnp.bfloat16),
        ]
        + [dma((experts,)) for _ in range(6)],
        compiler_params=pltpu.CompilerParams(
            collective_id=3, has_side_effects=True, vmem_limit_bytes=40 * 1024 * 1024
        ),
    )(attended, w_cols, residual, gain, router, placing)


def combine_kernel(
    experts, eo_ref, stream_ref, place_ref, share_ref, o_ref,
    low, arrived, final, e_send, e_recv, f_send, f_recv, local,
):
    group = lax.axis_index("expert")
    rows, cols = stream_ref.shape
    own_rows = rows // experts

    def target(k):
        return (group + k) % experts

    def slot(g):
        return pl.ds(pl.multiple_of(g * cols, 128), cols)

    def strip(g):
        return pl.ds(pl.multiple_of(g * own_rows, own_rows), own_rows)

    def give(k, g):
        return remote(
            low.at[:, slot(target(k))], arrived.at[g], e_send.at[k], e_recv.at[k], target(k), "expert"
        )

    def finish(k, g):
        return remote(
            final.at[strip(target(k)), :], o_ref.at[:, slot(g)], f_send.at[k], f_recv.at[k],
            target(k), "expert",
        )

    low[...] = eo_ref[...].astype(jnp.bfloat16)
    enter(0, 0, 0, experts)
    for k in range(experts - 1, 0, -1):
        give(k, group).start()
    own = pltpu.make_async_copy(low.at[:, slot(group)], arrived.at[group], local.at[0])
    own.start()
    own.wait()
    for k in range(1, experts):
        give(k, target(experts - k)).wait_recv()
    total = stream_ref[...]
    for g in range(experts):
        total = total + share_ref[:, g : g + 1] * jnp.dot(
            place_ref[g], arrived[g], preferred_element_type=jnp.float32
        )
    final[...] = total.astype(jnp.bfloat16)
    for k in range(experts - 1, 0, -1):
        finish(k, group).start()
    own = pltpu.make_async_copy(final.at[strip(group), :], o_ref.at[:, slot(group)], local.at[1])
    own.start()
    own.wait()
    for k in range(1, experts):
        finish(k, target(experts - k)).wait_recv()
    for k in range(1, experts):
        give(k, group).wait_send()
        finish(k, group).wait_send()


def combine(expert_out, stream, placing, shares):
    experts = lax.axis_size("expert")
    rows, cols = stream.shape
    capacity = expert_out.shape[0]
    vmem = pl.BlockSpec(memory_space=pltpu.VMEM)
    dma = pltpu.SemaphoreType.DMA
    return pl.pallas_call(
        functools.partial(combine_kernel, experts),
        out_shape=jax.ShapeDtypeStruct((rows // experts, cols * experts), jnp.bfloat16),
        in_specs=[vmem] * 4,
        out_specs=vmem,
        scratch_shapes=[
            pltpu.VMEM((capacity, cols * experts), jnp.bfloat16),
            pltpu.VMEM((experts, capacity, cols), jnp.bfloat16),
            pltpu.VMEM((rows, cols), jnp.bfloat16),
        ]
        + [dma((experts,)) for _ in range(4)]
        + [dma((2,))],
        compiler_params=pltpu.CompilerParams(
            collective_id=4, has_side_effects=True, vmem_limit_bytes=40 * 1024 * 1024
        ),
    )(expert_out, stream, placing, shares)


SPAN = 512
PARTS = 4


def expert_kernel(
    chips,
    tiles,
    spans,
    x_ref,
    wg_ref,
    wu_ref,
    wd_ref,
    o_ref,
    rows_in,
    hidden,
    keep,
    leaving,
    sib_in,
    part_in,
    ag_send,
    ag_recv,
    fw_send,
    fw_recv,
    sib_send,
    sib_recv,
    rs_send,
    rs_recv,
    local,
):
    j, f = pl.program_id(0), pl.program_id(1)
    me = lax.axis_index("blk")
    chip, core = me // 2, me % 2
    sibling = chip * 2 + 1 - core
    rows, width = x_ref.shape
    tile = wg_ref.shape[1]
    per_part = spans // PARTS
    wide = width // PARTS

    def push(k):
        return remote(
            rows_in.at[0, 0], rows_in.at[k, 0], ag_send.at[k], ag_recv.at[k], (chip + k) % chips * 2 + core
        )

    def forward(k):
        return remote(rows_in.at[k, 0], rows_in.at[k, 1], fw_send.at[k], fw_recv.at[k], sibling)

    def exchange(k, q):
        return remote(
            leaving.at[k % 2, q], sib_in.at[k, q], sib_send.at[k, q], sib_recv.at[k, q], sibling
        )

    def deliver(k, q):
        return remote(
            sib_in.at[k, q],
            part_in.at[k, q],
            rs_send.at[k, q],
            rs_recv.at[k, q],
            (chip + chips - k) % chips * 2 + core,
        )

    @pl.when((j == 0) & (f == 0))
    def _():
        own = pltpu.make_async_copy(x_ref, rows_in.at[0, 0], local)
        own.start()
        enter(chips, chip, core)
        own.wait()
        forward(0).start()
        for k in range(1, min(3, chips)):
            push(k).start()

    @pl.when((j >= 1) & (f == 0) & (j + 2 < chips))
    def _():
        push(j + 2).start()

    @pl.when(f == 0)
    def _():
        forward(j).wait_recv()

    def settle(k, q):
        exchange(k, q).wait_recv()
        part = pl.ds(pl.multiple_of(q * wide, wide), wide)

        @pl.when(k == 0)
        def _():
            o_ref[:, part] += sib_in[k, q].astype(jnp.float32)

        @pl.when(k > 0)
        def _():
            sib_in[k, q] = (keep[:, part] + sib_in[k, q].astype(jnp.float32)).astype(jnp.bfloat16)
            deliver(k, q).start()

    @pl.when((f == 1) & (j >= 1))
    def _():
        settle(j - 1, PARTS - 1)

    @pl.when(f < tiles)
    def _():
        tokens = rows_in[j].reshape(2 * rows, width)
        gate = jnp.dot(tokens, wg_ref[...], preferred_element_type=jnp.float32)
        up = jnp.dot(tokens, wu_ref[...], preferred_element_type=jnp.float32)
        hidden[:, pl.ds(pl.multiple_of(f * tile, tile), tile)] = (
            gate / (1.0 + jnp.exp(-gate)) * up
        ).astype(jnp.bfloat16)

    @pl.when((f == tiles // 2) & (j + 1 < chips))
    def _():
        push(j + 1).wait_recv()
        forward(j + 1).start()

    @pl.when(f >= tiles)
    def _():
        n = f - tiles
        q, r = n // per_part, n % per_part

        @pl.when((j >= 2) & (r == 0))
        def _():
            exchange(j - 2, q).wait_send()

        result = jnp.dot(hidden[...], wd_ref[...], preferred_element_type=jnp.float32)
        inner = pl.ds(pl.multiple_of(r * SPAN, SPAN), SPAN)
        outer = pl.ds(pl.multiple_of(n * SPAN, SPAN), SPAN)
        leaving[j % 2, q, :, inner] = result[rows:, :].astype(jnp.bfloat16)

        @pl.when(j == 0)
        def _():
            o_ref[:, outer] = result[:rows, :]

        @pl.when(j > 0)
        def _():
            keep[:, outer] = result[:rows, :]

        @pl.when(r == per_part - 1)
        def _():
            exchange(j, q).start()

            @pl.when(q >= 1)
            def _():
                settle(j, q - 1)

    @pl.when((j == chips - 1) & (f == tiles + spans - 1))
    def _():
        settle(chips - 1, PARTS - 1)
        for k in range(1, chips):
            for q in range(PARTS):
                deliver(k, q).wait_recv()
                o_ref[:, q * wide : (q + 1) * wide] += part_in[k, q].astype(jnp.float32)
        for k in range(chips):
            forward(k).wait_send()
            if k >= 1:
                push(k).wait_send()
                for q in range(PARTS):
                    deliver(k, q).wait_send()
        for k in range(max(0, chips - 2), chips):
            for q in range(PARTS):
                exchange(k, q).wait_send()


def expert_layer(x, gate_w, up_w, down_w):
    blocks = lax.axis_size("blk")
    chips = blocks // 2
    rows, width = x.shape
    units = gate_w.shape[1]
    tile = 256 if units % 256 == 0 else 128
    tiles = units // tile
    spans = width // SPAN
    dma = pltpu.SemaphoreType.DMA
    low, wide = jnp.bfloat16, jnp.float32
    return pl.pallas_call(
        functools.partial(expert_kernel, chips, tiles, spans),
        grid=(chips, tiles + spans),
        out_shape=jax.ShapeDtypeStruct((rows, width), wide),
        in_specs=[
            pl.BlockSpec(memory_space=pl.ANY),
            pl.BlockSpec((width, tile), lambda j, f: (0, jnp.minimum(f, tiles - 1))),
            pl.BlockSpec((width, tile), lambda j, f: (0, jnp.minimum(f, tiles - 1))),
            pl.BlockSpec((units, SPAN), lambda j, f: (0, jnp.maximum(f - tiles, 0))),
        ],
        out_specs=pl.BlockSpec((rows, width), lambda j, f: (0, 0)),
        scratch_shapes=[
            pltpu.VMEM((chips, 2, rows, width), low),
            pltpu.VMEM((2 * rows, units), low),
            pltpu.VMEM((rows, width), wide),
            pltpu.VMEM((2, PARTS, rows, width // PARTS), low),
            pltpu.VMEM((chips, PARTS, rows, width // PARTS), low),
            pltpu.VMEM((chips, PARTS, rows, width // PARTS), low),
        ]
        + [dma((chips,)) for _ in range(4)]
        + [dma((chips, PARTS)) for _ in range(4)]
        + [dma],
        compiler_params=pltpu.CompilerParams(
            collective_id=1,
            has_side_effects=True,
            dimension_semantics=("arbitrary", "arbitrary"),
            vmem_limit_bytes=60 * 1024 * 1024,
        ),
    )(x, gate_w, up_w, down_w)


def on_device(
    residual,
    queries,
    key_cache,
    value_cache,
    segments,
    routes,
    w_out,
    norm_gain,
    w_router,
    w_gate,
    w_up,
    w_down,
):
    tok_rows = queries.shape[0]
    kv_heads = key_cache.shape[1] // HD
    q_per_kv = H // KVH
    seq_block = lax.axis_index("blk")
    head_group = lax.axis_index("expert")
    first_row = seq_block * tok_rows
    query_pos = first_row + jnp.arange(tok_rows, dtype=jnp.int32)
    query_seg = lax.dynamic_slice_in_dim(segments, first_row, tok_rows)
    query_four = queries.reshape(tok_rows, kv_heads, q_per_kv, HD)
    score_scale = 1.0 / math.sqrt(HD)
    running = jnp.full((kv_heads, q_per_kv, tok_rows), -1e30, jnp.float32)
    key_rows, value_rows, w_part = gather_blocks(key_cache, value_cache, w_out)
    w_cols = lax.all_gather(w_part, "blk", axis=1, tiled=True)
    w_cols = w_cols.reshape(-1, w_cols.shape[2])
    piece_len = key_rows.shape[0]
    key_pos = jnp.arange(piece_len, dtype=jnp.int32)
    visible = (query_seg[:, None] == segments[None, :]) & (key_pos[None, :] <= query_pos[:, None])
    scores = (
        jnp.einsum(
            "qkgd,skd->kgqs",
            query_four,
            key_rows.reshape(piece_len, kv_heads, HD),
            preferred_element_type=jnp.float32,
        )
        * score_scale
    )
    scores = jnp.where(visible, scores, -1e30)
    newmax = jnp.maximum(running, jnp.max(scores, axis=-1))
    weights = jnp.where(visible, jnp.exp(scores - newmax[..., None]), 0.0)
    totals = jnp.sum(weights, axis=-1)
    weighted_sum = jnp.einsum(
        "kgqs,skd->kgqd",
        weights.astype(jnp.bfloat16),
        value_rows.reshape(piece_len, kv_heads, HD),
        preferred_element_type=jnp.float32,
    )
    running, totals, weighted_sum = (newmax, totals, weighted_sum)
    attended = (
        jnp.transpose(weighted_sum / totals[..., None], (2, 0, 1, 3))
        .reshape(tok_rows, kv_heads * q_per_kv * HD)
        .astype(jnp.bfloat16)
    )
    feat_width = residual.shape[1]
    experts = w_router.shape[1]
    first_col = head_group * feat_width
    capacity = tok_rows * TOP * 9 // (8 * experts)
    capacity = -(-capacity // 16) * 16
    ids = jnp.arange(experts, dtype=jnp.int32)
    picked = routes[:, :, None] == ids[None, None, :]
    routed = jnp.any(picked, axis=1).T
    slot_index = jnp.where(routed, jnp.cumsum(routed.astype(jnp.int32), axis=1) - 1, -1)
    slots = jnp.arange(capacity, dtype=jnp.int32)
    placing = (slot_index[:, None, :] == slots[None, :, None]).astype(jnp.bfloat16)
    placing_back = (slot_index[:, :, None] == slots[None, None, :]).astype(jnp.bfloat16)
    router = lax.dynamic_slice_in_dim(w_router, first_col, feat_width, 0).T
    router = jnp.pad(router, ((0, -experts % 16), (0, 0)))
    gain = lax.dynamic_slice_in_dim(norm_gain, first_col, feat_width)[None, :]
    attended = gather_heads(attended)
    stream, buffer, logits = mix_columns(attended, w_cols, residual, gain, router, placing)
    gate_score = jax.nn.sigmoid(logits[:experts, :].T)
    chosen = jnp.where(routed.T, gate_score, 0.0)
    shares = chosen / jnp.sum(chosen, axis=-1, keepdims=True)
    shares = jnp.pad(shares, ((0, 0), (0, -experts % 128)))
    expert_out = expert_layer(buffer, w_gate[0], w_up[0], w_down[0])
    return combine(expert_out, stream, placing_back, shares)


def solution(mesh):
    return jax.shard_map(
        on_device,
        mesh=mesh,
        in_specs=(
            P("blk", "expert"),
            P("blk", "expert"),
            P("blk", "expert"),
            P("blk", "expert"),
            P(),
            P("blk", None),
            P("expert", None),
            P(),
            P(),
            P("expert", None, "blk"),
            P("expert", None, "blk"),
            P("expert", "blk", None),
        ),
        out_specs=P(("blk", "expert"), None),
        check_vma=False,
    )
```
